32 devices in a mesh: ctx: 8 (over y, x, core), fsdp: 4 (over z).
Axes of the slice: x: 2, y: 2, z: 4, core: 2. Of those that a mesh axis runs over, the one named last changes fastest.
Arguments:
- layer_in: bfloat16 [4, 1024, 1600], P('fsdp', 'ctx'), may hold values from -6 to 6
- out_cot: bfloat16 [4, 1024, 1600], P('fsdp', 'ctx'), may hold values from -6 to 6
- first_gain: bfloat16 [1600], P('fsdp'), may hold values from 0.5 to 1.5
- first_bias: bfloat16 [1600], P('fsdp'), may hold values from -3 to 3
- qkv_weight: bfloat16 [1600, 4800], P('fsdp'), may hold values from -0.15625 to 0.15625
- qv_bias: bfloat16 [2, 1600], P(None, 'fsdp'), may hold values from -3 to 3
- out_weight: bfloat16 [1600, 1600], P('fsdp'), may hold values from -0.625 to 0.625
- out_bias: bfloat16 [1600], P('fsdp'), may hold values from -3 to 3
- second_gain: bfloat16 [1600], P('fsdp'), may hold values from 0.5 to 1.5
- second_bias: bfloat16 [1600], P('fsdp'), may hold values from -3 to 3
- fc_weight: bfloat16 [1600, 6400], P('fsdp'), may hold values from -0.15625 to 0.15625
- fc_bias: bfloat16 [6400], P('fsdp'), may hold values from -3 to 3
- proj_weight: bfloat16 [6400, 1600], P(None, 'fsdp'), may hold values from -0.078125 to 0.078125
- proj_bias: bfloat16 [1600], P('fsdp'), may hold values from -3 to 3
Outputs:
- layer_out: bfloat16 [4, 1024, 1600], P('fsdp', 'ctx')
- grad_in: bfloat16 [4, 1024, 1600], P('fsdp', 'ctx')
- grad_first_gain: float32 [1600], P('fsdp')
- grad_first_bias: float32 [1600], P('fsdp')
- grad_qkv_weight: float32 [1600, 4800], P('fsdp')
- grad_qv_bias: float32 [2, 1600], P(None, 'fsdp')
- grad_out_weight: float32 [1600, 1600], P('fsdp')
- grad_out_bias: float32 [1600], P('fsdp')
- grad_second_gain: float32 [1600], P('fsdp')
- grad_second_bias: float32 [1600], P('fsdp')
- grad_fc_weight: float32 [1600, 6400], P('fsdp')
- grad_fc_bias: float32 [6400], P('fsdp')
- grad_proj_weight: float32 [6400, 1600], P(None, 'fsdp')
- grad_proj_bias: float32 [1600], P('fsdp')
The draws below stay inside these ranges and needn't reach their ends.
All inputs are finite; a program needn't handle non-finite values.
Results may differ from the reference program's by a relative error of at most 0.03.
Values may be sent and summed in bfloat16 or wider, within the bound.
No kernel may reach another device: no remote copies, remote signals or barrier semaphores. Data moves between devices by JAX's collectives and lax.ppermute only.
A program may use at most 512 MiB of HBM per device.

```python
import math
import jax
import jax.numpy as jnp
from jax import lax

D = 1600
H = 25
HD = 64
FF = 6400
LEN = 1024
SEQS = 4
QBLOCK = 512


def levels(stream_key, shape, pieces, smallest, top_value):
    factor_of, own = 1.0, jax.random.fold_in(stream_key, 6)
    for dim, shards_of in pieces:
        steps = jnp.exp(jax.random.uniform(jax.random.fold_in(own, dim), (shards_of,), jnp.float32, smallest / len(pieces), top_value / len(pieces)))
        factor_of = factor_of * jnp.repeat(steps, shape[dim] // shards_of).reshape([-1 if axis == dim else 1 for axis in range(len(shape))])
    return factor_of


def bell_draw(stream_key, shape, scale, most, shards=(), held_as=jnp.bfloat16):
    values = scale * jax.random.normal(stream_key, shape, jnp.float32)
    if shards:
        values = values * levels(stream_key, shape, shards, -0.22, 0.18)
    return jnp.clip(values, -most, most).astype(held_as)


def setup_inputs(seed: int = 0) -> dict:
    streams_of = jax.random.split(jax.random.key(seed), 15)
    return {
        "layer_in": bell_draw(streams_of[0], (SEQS, LEN, D), 1.0, 6.0, ((0, 4), (1, 8))),
        "out_cot": bell_draw(streams_of[1], (SEQS, LEN, D), 1.0, 6.0, ((0, 4), (1, 8))),
        "first_gain": jnp.clip(1.0 + 0.1 * jax.random.normal(streams_of[2], (D,), jnp.float32), 0.5, 1.5).astype(jnp.bfloat16),
        "first_bias": bell_draw(streams_of[3], (D,), 0.5, 3.0, ((0, 4),)),
        "qkv_weight": bell_draw(streams_of[4], (D, 3 * D), D ** -0.5, 0.15625, ((0, 4),)),
        "qv_bias": bell_draw(streams_of[5], (2, D), 0.5, 3.0, ((1, 4),)),
        "out_weight": bell_draw(streams_of[6], (D, D), (D // 16) ** -0.5, 0.625, ((0, 4),)),
        "out_bias": bell_draw(streams_of[7], (D,), 0.5, 3.0, ((0, 4),)),
        "second_gain": jnp.clip(1.0 + 0.1 * jax.random.normal(streams_of[8], (D,), jnp.float32), 0.5, 1.5).astype(jnp.bfloat16),
        "second_bias": bell_draw(streams_of[9], (D,), 0.5, 3.0, ((0, 4),)),
        "fc_weight": bell_draw(streams_of[10], (D, FF), D ** -0.5, 0.15625, ((0, 4),)),
        "fc_bias": bell_draw(streams_of[11], (FF,), 0.5, 3.0, ((0, 4),)),
        "proj_weight": bell_draw(streams_of[12], (FF, D), FF ** -0.5, 0.078125, ((1, 4),)),
        "proj_bias": bell_draw(streams_of[13], (D,), 0.5, 3.0, ((0, 4),)),
    }


precise = lax.Precision.HIGHEST

@jax.custom_vjp
def low(v):
    return lax.optimization_barrier(v.astype(jnp.bfloat16)).astype(jnp.float32)

@jax.custom_vjp
def low_back(v):
    return v

def low_keep(v):
    return (low(v), None)

def low_pass(kept, grad):
    return (grad,)

def back_keep(v):
    return (v, None)

def back_low(kept, grad):
    return (low(grad),)
low.defvjp(low_keep, low_pass)
low_back.defvjp(back_keep, back_low)

def norm_apply(values, norm_gain, norm_bias):
    centre = lax.optimization_barrier(jnp.mean(values, axis=-1, keepdims=True))
    shifted = values - centre
    spread = lax.optimization_barrier(jnp.mean(shifted * shifted, axis=-1, keepdims=True))
    return shifted * lax.rsqrt(spread + 1e-05) * norm_gain + norm_bias

def attend_block(query_block, first_row, key_rows, value_rows):
    factor = 1.0 / math.sqrt(HD)
    raw_scores = factor * jnp.einsum('qhd,khd->hqk', query_block, key_rows, precision=precise)
    scores = low_back(raw_scores)
    query_pos = first_row + jnp.arange(QBLOCK, dtype=jnp.int32)
    key_pos = jnp.arange(LEN, dtype=jnp.int32)
    allowed = key_pos[None, :] <= query_pos[:, None]
    masked = jnp.where(allowed[None], scores, -1e+30)
    row_max = lax.optimization_barrier(jnp.max(masked, axis=-1, keepdims=True))
    weights = jnp.where(allowed[None], jnp.exp(masked - row_max), 0.0)
    probs = weights / lax.optimization_barrier(jnp.sum(weights, axis=-1, keepdims=True))
    return jnp.einsum('hqk,khd->qhd', probs, value_rows, precision=precise)

def forward(layer_in, first_gain, first_bias, qkv_weight, qv_bias, out_weight, out_bias, second_gain, second_bias, fc_weight, fc_bias, proj_weight, proj_bias):
    tokens = layer_in.reshape(SEQS * LEN, D)
    normed_one = low(norm_apply(tokens, first_gain, first_bias))
    projected = jnp.dot(normed_one, qkv_weight, precision=precise)
    queries = low_back(low(projected[:, 0:D] + qv_bias[0]))
    key_rows = low_back(low(projected[:, D:2 * D]))
    value_rows = low_back(low(projected[:, 2 * D:3 * D] + qv_bias[1]))
    block_fn = jax.checkpoint(attend_block)

    def one_sequence(packed):
        query_seq, key_seq, value_seq = packed
        query_blocks = query_seq.reshape(LEN // QBLOCK, QBLOCK, H, HD)
        starts = jnp.arange(LEN // QBLOCK, dtype=jnp.int32) * QBLOCK
        result = lax.map(lambda paired: block_fn(paired[0], paired[1], key_seq, value_seq), (query_blocks, starts))
        return result.reshape(LEN, H, HD)
    attn_f = lax.map(one_sequence, (queries.reshape(SEQS, LEN, H, HD), key_rows.reshape(SEQS, LEN, H, HD), value_rows.reshape(SEQS, LEN, H, HD)))
    attn_out = low_back(low(attn_f.reshape(SEQS * LEN, D)))
    branch = low_back(jnp.dot(attn_out, out_weight, precision=precise) + out_bias)
    resid = tokens + branch
    normed_two = low(norm_apply(resid, second_gain, second_bias))
    pre_act = low_back(jnp.dot(normed_two, fc_weight, precision=precise) + fc_bias)
    activated = low(jax.nn.gelu(pre_act, approximate=True))
    mlp_out = jnp.dot(activated, proj_weight, precision=precise) + proj_bias
    return (resid + mlp_out).reshape(SEQS, LEN, D)

def reference(layer_in, out_cot, first_gain, first_bias, qkv_weight, qv_bias, out_weight, out_bias, second_gain, second_bias, fc_weight, fc_bias, proj_weight, proj_bias):
    f32 = jnp.float32
    result, pullback = jax.vjp(forward, layer_in.astype(f32), first_gain.astype(f32), first_bias.astype(f32), qkv_weight.astype(f32), qv_bias.astype(f32), out_weight.astype(f32), out_bias.astype(f32), second_gain.astype(f32), second_bias.astype(f32), fc_weight.astype(f32), fc_bias.astype(f32), proj_weight.astype(f32), proj_bias.astype(f32))
    grads = pullback(out_cot.astype(f32))
    return (result.astype(jnp.bfloat16), grads[0].astype(jnp.bfloat16), grads[1], grads[2], grads[3], grads[4], grads[5], grads[6], grads[7], grads[8], grads[9], grads[10], grads[11], grads[12])
```

```python
import math

import jax
import jax.numpy as jnp
from jax import lax
from jax.experimental import pallas as pl
from jax.experimental.pallas import tpu as pltpu
from jax.sharding import PartitionSpec as P

H = 25
HD = 64
ROWS = 256

f32 = jnp.float32
bf16 = jnp.bfloat16


def norm_apply(values, norm_gain, norm_bias):
    centre = jnp.mean(values, axis=-1, keepdims=True)
    shifted = values - centre
    spread = jnp.mean(shifted * shifted, axis=-1, keepdims=True)
    return shifted * lax.rsqrt(spread + 1e-05) * norm_gain + norm_bias


def matmul(left, right, left_dim, right_dim):
    return lax.dot_general(
        left, right, (((left_dim,), (right_dim,)), ((), ())), preferred_element_type=f32
    )


class Plane:
    def __init__(self, size):
        self.size = size
        self.chips = size // 2
        self.wide = math.isqrt(self.chips)
        self.tall = self.chips // self.wide
        self.shifts = [(da, db) for da in range(self.tall) for db in range(self.wide)]
        self.me = lax.axis_index("ctx")

    def _moved(self, chip, shift, sign):
        row, col = chip // self.wide, chip % self.wide
        row = (row + sign * shift[0] + self.tall) % self.tall
        col = (col + sign * shift[1] + self.wide) % self.wide
        return row * self.wide + col

    def index_of(self, slot):
        core = self.me % 2
        if slot >= self.chips:
            core = 1 - core
        return self._moved(self.me // 2, self.shifts[slot % self.chips], -1) * 2 + core

    def from_slot(self, value, slot):
        return lax.ppermute(value, "ctx", self._pairs(slot, 1))

    def to_slot(self, value, slot):
        return lax.ppermute(value, "ctx", self._pairs(slot, -1))

    def _pairs(self, slot, sign):
        shift, flip = self.shifts[slot % self.chips], slot // self.chips
        return [
            (i, self._moved(i // 2, shift, sign) * 2 + (i % 2 + flip) % 2)
            for i in range(self.size)
        ]

    def opposite(self, slot):
        da, db = self.shifts[slot % self.chips]
        shift = ((self.tall - da) % self.tall, (self.wide - db) % self.wide)
        return self.shifts.index(shift) + self.chips * (slot // self.chips)

    def swap(self, value):
        return self.to_slot(value, self.chips)

    def gather(self, value):
        mine = jnp.concatenate(
            [value] + [self.from_slot(value, slot) for slot in range(1, self.chips)], axis=0
        )
        return jnp.concatenate([mine, self.swap(mine)], axis=0)

    def scatter(self, mine, theirs):
        total = mine + self.swap(theirs.astype(bf16)).astype(f32)
        total = total.reshape((self.chips, -1) + mine.shape[1:])
        sent = total[1:].astype(bf16)
        result = total[0]
        for slot in range(1, self.chips):
            result = result + self.to_slot(sent[slot - 1], slot).astype(f32)
        return result


def line_gather(value, size):
    at = lax.axis_index("fsdp")
    rows = value.shape[0]
    zeros = (0,) * (value.ndim - 1)

    def put(whole, part, block):
        return lax.dynamic_update_slice(whole, part, (block * rows,) + zeros)

    whole = jnp.zeros((size * rows,) + value.shape[1:], value.dtype)
    if size != 4:
        whole = put(whole, value, at)
        for step in range(1, size):
            moved = lax.ppermute(value, "fsdp", [(i, (i + step) % size) for i in range(size)])
            whole = put(whole, moved, (at - step) % size)
        return whole
    up = lax.ppermute(value, "fsdp", [(0, 1), (1, 2), (2, 3)])
    down = lax.ppermute(value, "fsdp", [(1, 0), (2, 1), (3, 2)])
    cross = lax.ppermute(value, "fsdp", [(0, 2), (1, 3), (2, 0), (3, 1)])
    relay = lax.ppermute(cross, "fsdp", [(2, 3), (1, 0)])
    whole = put(whole, up, (at + 3) % 4)
    whole = put(whole, down, (at + 1) % 4)
    whole = put(whole, cross, (at + 2) % 4)
    whole = put(whole, relay, jnp.where(at == 0, 3, jnp.where(at == 3, 0, at)))
    return put(whole, value, at)


def line_scatter(parts, size):
    at = lax.axis_index("fsdp")

    def part(block):
        return lax.dynamic_index_in_dim(parts, block % size, 0, keepdims=False)

    result = part(at)
    if size != 4:
        for step in range(1, size):
            moved = lax.ppermute(
                part(at + step).astype(bf16), "fsdp", [(i, (i + step) % size) for i in range(size)]
            )
            result = result + moved.astype(f32)
        return result
    relay = lax.ppermute(part(3 - at).astype(bf16), "fsdp", [(0, 1), (3, 2)])
    up = lax.ppermute(part(at + 1).astype(bf16), "fsdp", [(0, 1), (1, 2), (2, 3)])
    down = lax.ppermute(part(at + 3).astype(bf16), "fsdp", [(1, 0), (2, 1), (3, 2)])
    cross = part(at + 2) + relay.astype(f32)
    cross = lax.ppermute(cross.astype(bf16), "fsdp", [(0, 2), (1, 3), (2, 0), (3, 1)])
    return result + up.astype(f32) + down.astype(f32) + cross.astype(f32)


def _blocks(length):
    count = length // ROWS
    return count, count <= 4


def _scores_t(key_head, query_block, first, length):
    scores = matmul(key_head, query_block, 1, 1)
    key_at = lax.broadcasted_iota(jnp.int32, scores.shape, 0)
    query_at = lax.broadcasted_iota(jnp.int32, scores.shape, 1) + first
    return scores, key_at <= query_at


def forward_kernel(heads, places, q_ref, k_ref, v_ref, out_ref, out_t_ref, log_ref, q_s, k_s, v_s):
    length = q_ref.shape[0]
    slots = places.shape[0]
    rows = length // slots
    for slot in range(slots):
        to = pl.ds(pl.multiple_of(places[slot] * rows, rows), rows)
        at = pl.ds(slot * rows, rows)
        q_s[to, :] = q_ref[at, :]
        k_s[to, :] = k_ref[at, :]
        v_s[to, :] = v_ref[at, :]

    count, few = _blocks(length)
    for head in range(heads):
        cols = slice(head * HD, (head + 1) * HD)

        def block(index, head=head, cols=cols):
            first = index * ROWS
            until = first + ROWS if few else length
            query = q_s[pl.ds(first, ROWS), cols]
            scores, kept = _scores_t(k_s[0:until, cols], query, first, length)
            scores = jnp.where(kept, scores, -1e30)
            top = jnp.max(scores, axis=0, keepdims=True)
            weights = jnp.exp(scores - top)
            total = jnp.sum(weights, axis=0, keepdims=True)
            summed = matmul(v_s[0:until, cols].T, weights.astype(bf16), 1, 0)
            out_t_ref[cols, pl.ds(first, ROWS)] = summed / total
            log_ref[head : head + 1, pl.ds(first, ROWS)] = top + jnp.log(total)

        if few:
            for index in range(count):
                block(index)
        else:
            lax.fori_loop(0, count, lambda i, c: (block(i), c)[1], 0)
    q_s[...] = out_t_ref[...].T.astype(bf16)
    for slot in range(slots):
        to = pl.ds(pl.multiple_of(places[slot] * rows, rows), rows)
        out_ref[pl.ds(slot * rows, rows), :] = q_s[to, :]


def backward_kernel(
    heads, places, q_ref, k_ref, v_ref, d_ref, out_t_ref, log_ref, g_ref,
    q_s, k_s, v_s, d_s, dk_s, dv_s, dq_t
):
    length = q_ref.shape[0]
    slots = places.shape[0]
    rows = length // slots
    width = heads * HD
    for slot in range(slots):
        to = pl.ds(pl.multiple_of(places[slot] * rows, rows), rows)
        at = pl.ds(slot * rows, rows)
        q_s[to, :] = q_ref[at, :]
        k_s[to, :] = k_ref[at, :]
        v_s[to, :] = v_ref[at, :]
        d_s[to, :] = d_ref[at, :]
    dk_s[...] = jnp.zeros_like(dk_s)
    dv_s[...] = jnp.zeros_like(dv_s)
    count, few = _blocks(length)
    for head in range(heads):
        cols = slice(head * HD, (head + 1) * HD)

        def block(index, head=head, cols=cols):
            first = index * ROWS
            until = first + ROWS if few else length
            at = pl.ds(first, ROWS)
            query = q_s[at, cols]
            cot = d_s[at, cols]
            delta = jnp.sum(cot.astype(f32).T * out_t_ref[cols, at], axis=0, keepdims=True)
            scores, kept = _scores_t(k_s[0:until, cols], query, first, length)
            weights = jnp.where(kept, jnp.exp(scores - log_ref[head : head + 1, at]), 0.0)
            d_weights = matmul(v_s[0:until, cols], cot, 1, 1)
            d_scores = (weights * (d_weights - delta)).astype(bf16)
            dv_s[head, 0:until, :] += matmul(weights.astype(bf16), cot, 1, 0)
            dk_s[head, 0:until, :] += matmul(d_scores, query, 1, 0)
            dq_t[cols, at] = matmul(k_s[0:until, cols].T, d_scores, 1, 0)

        if few:
            for index in range(count):
                block(index)
        else:
            lax.fori_loop(0, count, lambda i, c: (block(i), c)[1], 0)
    scale = 1.0 / math.sqrt(HD)
    q_s[...] = (dq_t[...] * scale).T.astype(bf16)
    for head in range(heads):
        cols = slice(head * HD, (head + 1) * HD)
        k_s[:, cols] = dk_s[head].astype(bf16)
        v_s[:, cols] = dv_s[head].astype(bf16)
    for slot in range(slots):
        to = pl.ds(pl.multiple_of(places[slot] * rows, rows), rows)
        at = pl.ds(slot * rows, rows)
        g_ref[at, 0:width] = q_s[to, :]
        g_ref[at, width : 2 * width] = k_s[to, :]
        g_ref[at, 2 * width : 3 * width] = v_s[to, :]


VMEM = pl.BlockSpec(memory_space=pltpu.VMEM)
SMEM = pl.BlockSpec(memory_space=pltpu.SMEM)


def attend(heads, places, query, key, value):
    length, width = query.shape
    return pl.pallas_call(
        lambda *refs: forward_kernel(heads, *refs),
        out_shape=(
            jax.ShapeDtypeStruct((length, width), bf16),
            jax.ShapeDtypeStruct((width, length), f32),
            jax.ShapeDtypeStruct((heads, length), f32),
        ),
        in_specs=[SMEM, VMEM, VMEM, VMEM],
        out_specs=(VMEM, VMEM, VMEM),
        scratch_shapes=[pltpu.VMEM((length, width), bf16)] * 3,
        name="attend",
    )(places, query, key, value)


def attend_back(heads, places, query, key, value, cot, out_t, log_total):
    length, width = query.shape
    return pl.pallas_call(
        lambda *refs: backward_kernel(heads, *refs),
        out_shape=jax.ShapeDtypeStruct((length, 3 * width), bf16),
        in_specs=[SMEM] + [VMEM] * 6,
        out_specs=VMEM,
        scratch_shapes=[pltpu.VMEM((length, width), bf16)] * 4
        + [pltpu.VMEM((heads, length, HD), f32)] * 2
        + [pltpu.VMEM((width, length), f32)],
        name="attend_back",
    )(places, query, key, value, cot, out_t, log_total)


def on_device(
    layer_in, out_cot, first_gain, first_bias, qkv_weight, qv_bias, out_weight, out_bias,
    second_gain, second_bias, fc_weight, fc_bias, proj_weight, proj_bias
):
    size = lax.axis_size("ctx")
    line = lax.axis_size("fsdp")
    plane = Plane(size)
    me = plane.me
    tokens = layer_in[0].astype(f32)
    rows, width = tokens.shape
    piece = width // line
    hidden = fc_weight.shape[1]
    part = hidden // size
    heads = -(-H // size)
    span = heads * HD
    spread = size * span
    share = -(-(-(-piece // size)) // 8) * 8
    slots = range(size)
    places = jnp.stack([plane.index_of(slot) for slot in slots]).astype(jnp.int32)
    slot_of = [0] * size
    order = jnp.zeros((size,), jnp.int32)
    order = order.at[places].set(jnp.arange(size, dtype=jnp.int32))

    vectors = jnp.concatenate(
        [
            first_gain[None], first_bias[None], qv_bias, out_bias[None], second_gain[None],
            second_bias[None], proj_bias[None], fc_bias.reshape(-1, piece),
        ],
        axis=0,
    )
    count = vectors.shape[0]
    vectors = line_gather(vectors, line).reshape(line, count, piece).astype(f32)
    gain_one, bias_one, bias_q, bias_v, bias_out, gain_two, bias_two, bias_proj = (
        vectors[:, i].reshape(width) for i in range(8)
    )
    bias_fc = vectors[:, 8:].reshape(hidden)
    bias_fc = lax.dynamic_slice_in_dim(bias_fc, me * part, part)

    def heads_of(vector):
        padded = jnp.pad(vector, ((0, spread - width),))
        return lax.dynamic_slice_in_dim(padded, me * span, span)

    padded = jnp.pad(qkv_weight, ((0, 0), (0, spread - width)))
    own_qkv = jnp.concatenate(
        [
            lax.dynamic_slice_in_dim(padded, i * width + me * span, span, axis=1)
            for i in range(3)
        ],
        axis=1,
    )
    full_qkv = line_gather(own_qkv, line)
    padded = jnp.pad(out_weight, ((0, size * share - piece), (0, 0)))
    own_out = lax.dynamic_slice_in_dim(padded, me * share, share, axis=0)
    all_out = line_gather(own_out, line)
    own_fc = lax.dynamic_slice_in_dim(fc_weight, me * part, part, axis=1)
    full_fc = line_gather(own_fc, line)
    own_proj = lax.dynamic_slice_in_dim(proj_weight, me * part, part, axis=0).T
    full_proj = line_gather(own_proj, line)

    normed_one = norm_apply(tokens, gain_one, bias_one).astype(bf16)
    normed_one = plane.gather(normed_one)
    projected = matmul(normed_one, full_qkv, 1, 0)
    scale = 1.0 / math.sqrt(HD)
    queries = (projected[:, 0:span] + heads_of(bias_q)).astype(bf16) * jnp.asarray(scale, bf16)
    keys = projected[:, span : 2 * span].astype(bf16)
    values = (projected[:, 2 * span :] + heads_of(bias_v)).astype(bf16)
    attn_heads, attn_t, log_total = attend(heads, places, queries, keys, values)

    def to_tokens(by_slot):
        got = [None] * size
        got[0] = by_slot[0]
        for slot in range(1, size):
            got[plane.opposite(slot)] = plane.to_slot(by_slot[slot], slot)
        got = jnp.stack(got)
        got = [lax.dynamic_index_in_dim(got, order[i], 0, keepdims=False) for i in range(size)]
        return jnp.concatenate(got, axis=1)[:, :width]

    def to_heads(by_token):
        by_token = jnp.pad(by_token, ((0, 0), (0, spread - width)))
        got = [None] * size
        for slot in range(size):
            block = lax.dynamic_slice_in_dim(by_token, places[slot] * span, span, axis=1)
            got[plane.opposite(slot)] = plane.to_slot(block, slot) if slot else block
        return jnp.concatenate(got, axis=0)

    attn_out = to_tokens(attn_heads.reshape(size, rows, span))
    all_out = plane.gather(all_out[None])
    all_out = jnp.concatenate(
        [
            lax.dynamic_index_in_dim(all_out, order[i], 0).reshape(line, share, width)
            for i in range(size)
        ],
        axis=1,
    )
    full_out = all_out[:, :piece].reshape(width, width)
    resid = tokens + matmul(attn_out, full_out, 1, 0) + bias_out

    cotangent = out_cot[0]
    all_cot = plane.gather(cotangent)
    normed_two = norm_apply(resid, gain_two, bias_two).astype(bf16)
    normed_two = plane.gather(normed_two)
    pre_act = matmul(normed_two, full_fc, 1, 0) + bias_fc
    activated, gelu_back = jax.vjp(lambda v: jax.nn.gelu(v, approximate=True), pre_act)
    activated = activated.astype(bf16)
    half = size // 2 * rows
    mlp_theirs = matmul(activated[half:], full_proj, 1, 1)
    mlp_mine = matmul(activated[:half], full_proj, 1, 1)
    d_activated = matmul(all_cot, full_proj, 1, 0)
    d_pre = gelu_back(d_activated)[0].astype(bf16)
    norm_theirs = matmul(d_pre[half:], full_fc, 1, 1)
    norm_mine = matmul(d_pre[:half], full_fc, 1, 1)
    d_norm_two = plane.scatter(norm_mine, norm_theirs)
    grad_proj = matmul(all_cot, activated, 0, 0).reshape(line, piece, part)
    grad_fc = matmul(normed_two, d_pre, 0, 0).reshape(line, piece, part)
    layer_out = plane.scatter(mlp_mine, mlp_theirs) + resid + bias_proj
    layer_out = layer_out.astype(bf16)[None]

    unused_two, norm_back_two = jax.vjp(norm_apply, resid, gain_two, bias_two)
    d_resid_norm, grad_gain_two, grad_bias_two = norm_back_two(d_norm_two)
    cot_float = cotangent.astype(f32)
    d_resid = cot_float + d_resid_norm
    d_branch = d_resid.astype(bf16)

    d_attn = matmul(d_branch, full_out, 1, 1).astype(bf16)
    d_attn = to_heads(d_attn)
    grads = attend_back(heads, places, queries, keys, values, d_attn, attn_t, log_total)
    grad_qkv = matmul(normed_one, grads, 0, 0).reshape(line, piece, 3 * span)
    d_theirs = matmul(grads[half:], full_qkv, 1, 1)
    d_mine = matmul(grads[:half], full_qkv, 1, 1)
    d_norm_one = plane.scatter(d_mine, d_theirs)
    unused_one, norm_back_one = jax.vjp(norm_apply, tokens, gain_one, bias_one)
    d_in_norm, grad_gain_one, grad_bias_one = norm_back_one(d_norm_one)
    grad_in = (d_resid + d_in_norm).astype(bf16)[None]

    def spread_out(value):
        value = plane.gather(value.astype(bf16)[None])
        return [lax.dynamic_index_in_dim(value, order[i], 0, keepdims=False) for i in range(size)]

    grad_proj = spread_out(line_scatter(grad_proj, line).T)
    grad_proj = jnp.concatenate(grad_proj, axis=0).astype(f32)
    grad_fc = spread_out(line_scatter(grad_fc, line))
    grad_fc = jnp.concatenate(grad_fc, axis=1).astype(f32)
    grad_qkv = spread_out(line_scatter(grad_qkv, line))
    grad_qkv = jnp.concatenate(
        [
            jnp.concatenate([g[:, i * span : (i + 1) * span] for g in grad_qkv], axis=1)[:, :width]
            for i in range(3)
        ],
        axis=1,
    ).astype(f32)

    grad_out = matmul(attn_out, d_branch, 0, 0).reshape(line, piece, width)
    grad_out = jnp.pad(grad_out, ((0, 0), (0, size * share - piece), (0, 0)))
    grad_out = grad_out.reshape(line, size, share, width)
    by_slot = [
        lax.dynamic_index_in_dim(grad_out, places[i], 1, keepdims=False) for i in range(size)
    ]
    mine = jnp.concatenate(by_slot[: size // 2], axis=0).reshape(size // 2 * line * share, width)
    theirs = jnp.concatenate(by_slot[size // 2 :], axis=0).reshape(mine.shape)
    grad_out = plane.scatter(mine, theirs).reshape(line, share, width)
    grad_out = spread_out(line_scatter(grad_out, line))
    grad_out = jnp.concatenate(grad_out, axis=0)[:piece].astype(f32)

    def summed(value):
        return jnp.sum(value.astype(f32), axis=0)

    vectors = jnp.concatenate(
        [
            grad_gain_one, grad_bias_one, summed(d_branch), grad_gain_two, grad_bias_two,
            summed(cot_float), summed(grads[:, :span]), summed(grads[:, 2 * span :]),
            summed(d_pre),
        ]
    )
    vectors = plane.gather(vectors[None])
    by_token = jnp.sum(vectors[:, : 6 * width], axis=0).reshape(6, line, piece)
    vectors = jnp.take(vectors, order, axis=0)[:, 6 * width :]
    bias_parts = jnp.stack(
        [vectors[:, i * span : (i + 1) * span].reshape(spread)[:width] for i in range(2)]
    ).reshape(2, line, piece)
    hidden_part = vectors[:, 2 * span :].reshape(line, hidden // line)
    parts = jnp.concatenate(
        [
            by_token.transpose(1, 0, 2).reshape(line, 6 * piece),
            bias_parts.transpose(1, 0, 2).reshape(line, 2 * piece),
            hidden_part,
        ],
        axis=1,
    )
    final = line_scatter(parts, line)
    singles = [final[i * piece : (i + 1) * piece] for i in range(8)]
    return (
        layer_out,
        grad_in,
        singles[0],
        singles[1],
        grad_qkv,
        jnp.stack(singles[6:8]),
        grad_out,
        singles[2],
        singles[3],
        singles[4],
        grad_fc,
        final[8 * piece :],
        grad_proj,
        singles[5],
    )


def solution(mesh):
    by_width = P("fsdp")
    tokens = P("fsdp", "ctx", None)
    matrix = P("fsdp", None)
    across = P(None, "fsdp")
    params = (
        by_width, by_width, matrix, across, matrix, by_width, by_width, by_width, matrix, by_width,
        across, by_width,
    )
    return jax.shard_map(
        on_device,
        mesh=mesh,
        in_specs=(tokens, tokens) + params,
        out_specs=(tokens, tokens) + params,
        check_vma=False,
    )
```

```python
import math

import jax
import jax.numpy as jnp
from jax import lax
from jax.experimental import pallas as pl
from jax.experimental.pallas import tpu as pltpu
from jax.sharding import PartitionSpec as P

H = 25
HD = 64
ROWS = 256

f32 = jnp.float32
bf16 = jnp.bfloat16

VMEM = pl.BlockSpec(memory_space=pltpu.VMEM)
SMEM = pl.BlockSpec(memory_space=pltpu.SMEM)
ANY = pl.BlockSpec(memory_space=pl.ANY)


def shape(*dims, dtype=bf16):
    return jax.ShapeDtypeStruct(dims, dtype)


def matmul(left, right, left_dim, right_dim):
    return lax.dot_general(
        left, right, (((left_dim,), (right_dim,)), ((), ())), preferred_element_type=f32
    )


def norm_parts(values):
    centre = jnp.mean(values, axis=-1, keepdims=True)
    shifted = values - centre
    spread = jnp.mean(shifted * shifted, axis=-1, keepdims=True)
    inverse = lax.rsqrt(spread + 1e-05)
    return shifted * inverse, inverse


def norm_back(cot, values, gain):
    normal, inverse = norm_parts(values)
    scaled = cot * gain
    first = jnp.mean(scaled, axis=-1, keepdims=True)
    second = jnp.mean(scaled * normal, axis=-1, keepdims=True)
    back = inverse * (scaled - first - normal * second)
    return (
        back,
        jnp.sum(cot * normal, axis=0, keepdims=True),
        jnp.sum(cot, axis=0, keepdims=True),
    )


class Plane:
    def __init__(self, size):
        self.size = size
        self.chips = size // 2
        self.wide = math.isqrt(self.chips)
        self.tall = self.chips // self.wide
        self.shifts = [(da, db) for da in range(self.tall) for db in range(self.wide)]
        self.me = lax.axis_index("ctx")
        places = [self.index_of(slot) for slot in range(size)]
        self.places = jnp.stack(places).astype(jnp.int32)

    def _moved(self, chip, shift, sign):
        row, col = chip // self.wide, chip % self.wide
        row = (row + sign * shift[0] + self.tall) % self.tall
        col = (col + sign * shift[1] + self.wide) % self.wide
        return row * self.wide + col

    def index_of(self, slot):
        core = self.me % 2
        if slot >= self.chips:
            core = 1 - core
        return self._moved(self.me // 2, self.shifts[slot % self.chips], -1) * 2 + core

    def _pairs(self, slot, sign):
        shift, flip = self.shifts[slot % self.chips], slot // self.chips
        return [
            (i, self._moved(i // 2, shift, sign) * 2 + (i % 2 + flip) % 2)
            for i in range(self.size)
        ]

    def from_slot(self, value, slot):
        return lax.ppermute(value, "ctx", self._pairs(slot, 1))

    def to_slot(self, value, slot):
        return lax.ppermute(value, "ctx", self._pairs(slot, -1))

    def opposite(self, slot):
        da, db = self.shifts[slot % self.chips]
        shift = ((self.tall - da) % self.tall, (self.wide - db) % self.wide)
        return self.shifts.index(shift) + self.chips * (slot // self.chips)

    def swap(self, value):
        return self.to_slot(value, self.chips)

    def gather(self, value):
        mine = [value] + [self.from_slot(value, slot) for slot in range(1, self.chips)]
        return mine + [self.swap(piece) for piece in mine]

    def exchange(self, pieces):
        got = [pieces[0]] + [None] * (self.size - 1)
        for slot in range(1, self.size):
            got[self.opposite(slot)] = self.to_slot(pieces[slot], slot)
        return got

    def scatter(self, mine, theirs):
        received = self.swap(theirs)
        chips, dims = self.chips, mine.shape[1:]

        def kernel(places, mine_ref, received_ref, own_ref, *sent):
            def total(slot):
                chip = places[slot] // 2
                return mine_ref[chip].astype(f32) + received_ref[chip].astype(f32)

            own_ref[...] = total(0)
            for slot in range(1, chips):
                sent[slot - 1][...] = total(slot).astype(bf16)

        own, *sent = pl.pallas_call(
            kernel,
            out_shape=[shape(*dims, dtype=f32)] + [shape(*dims)] * (chips - 1),
            in_specs=[SMEM, VMEM, VMEM],
            out_specs=[VMEM] * chips,
            name="pair_sum",
        )(self.places, mine, received)
        return [own] + [self.to_slot(sent[slot - 1], slot) for slot in range(1, chips)]

    def collect(self, pieces):
        dims = pieces[0].shape
        count = len(pieces)

        def kernel(places, *refs):
            parts, out, sems = refs[:count], refs[count], refs[count + 1]
            copies = [
                pltpu.make_async_copy(parts[i], out.at[places[i]], sems.at[i])
                for i in range(count)
            ]
            for copy in copies:
                copy.start()
            for copy in copies:
                copy.wait()

        return pl.pallas_call(
            kernel,
            out_shape=shape(count, *dims, dtype=pieces[0].dtype),
            in_specs=[SMEM] + [ANY] * count,
            out_specs=ANY,
            scratch_shapes=[pltpu.SemaphoreType.DMA((count,))],
            name="collect",
        )(self.places, *pieces)


def line_gather(value, size):
    at = lax.axis_index("fsdp")
    if size != 4:
        return lax.all_gather(value, "fsdp", axis=0, tiled=True)
    up = lax.ppermute(value, "fsdp", [(0, 1), (1, 2), (2, 3)])
    down = lax.ppermute(value, "fsdp", [(1, 0), (2, 1), (3, 2)])
    cross = lax.ppermute(value, "fsdp", [(0, 2), (1, 3), (2, 0), (3, 1)])
    relay = lax.ppermute(cross, "fsdp", [(2, 3), (1, 0)])
    rows = value.shape[0]

    def kernel(at_ref, own_ref, up_ref, down_ref, cross_ref, relay_ref, out_ref, sems):
        here = at_ref[0]

        def copy(ref, block, sem):
            to = pl.ds(pl.multiple_of(block * rows, rows), rows)
            return pltpu.make_async_copy(ref, out_ref.at[to], sems.at[sem])

        steps = [
            (None, copy(own_ref, here, 0)),
            (None, copy(cross_ref, (here + 2) % 4, 1)),
            (here == 0, copy(relay_ref, 3, 2)),
            (here != 0, copy(up_ref, (here + 3) % 4, 2)),
            (here == 3, copy(relay_ref, 0, 3)),
            (here != 3, copy(down_ref, (here + 1) % 4, 3)),
        ]
        for act in (lambda c: c.start(), lambda c: c.wait()):
            for when, step in steps:
                if when is None:
                    act(step)
                else:
                    pl.when(when)(lambda step=step, act=act: act(step))

    return pl.pallas_call(
        kernel,
        out_shape=shape(size * rows, value.shape[1]),
        in_specs=[SMEM] + [ANY] * 5,
        out_specs=ANY,
        scratch_shapes=[pltpu.SemaphoreType.DMA((4,))],
        name="line_collect",
    )(at.astype(jnp.int32)[None], value, up, down, cross, relay)


def line_scatter(parts):
    return lax.psum_scatter(parts, "fsdp", scatter_dimension=0, tiled=False)


def _blocks(length):
    count = length // ROWS
    return count, count <= 4


def _scores(key_head, query_block, first):
    scores = matmul(key_head, query_block, 1, 1)
    key_at = lax.broadcasted_iota(jnp.int32, scores.shape, 0)
    query_at = lax.broadcasted_iota(jnp.int32, scores.shape, 1) + first
    return scores, key_at <= query_at


def _sweep(length, block):
    count, few = _blocks(length)
    if few:
        for index in range(count):
            block(index, (index + 1) * ROWS)
    else:
        lax.fori_loop(0, count, lambda i, c: (block(i, length), c)[1], 0)


def attend(heads, plane, query, key, value):
    length, width = query.shape
    slots = plane.size
    rows = length // slots

    def kernel(places, q_ref, k_ref, v_ref, *refs):
        outs, (out_t_ref, log_ref, o_s) = refs[:slots], refs[slots:]
        for head in range(heads):
            cols = slice(head * HD, (head + 1) * HD)

            def block(index, until, head=head, cols=cols):
                at = pl.ds(index * ROWS, ROWS)
                scores, kept = _scores(k_ref[0:until, cols], q_ref[at, cols], index * ROWS)
                scores = jnp.where(kept, scores, -1e30)
                top = jnp.max(scores, axis=0, keepdims=True)
                weights = jnp.exp(scores - top)
                total = jnp.sum(weights, axis=0, keepdims=True)
                summed = matmul(v_ref[0:until, cols].T, weights.astype(bf16), 1, 0)
                out_t_ref[cols, at] = summed / total
                log_ref[head : head + 1, at] = top + jnp.log(total)

            _sweep(length, block)
        o_s[...] = out_t_ref[...].T.astype(bf16)
        for slot in range(slots):
            outs[slot][...] = o_s[pl.ds(pl.multiple_of(places[slot] * rows, rows), rows), :]

    *pieces, out_t, log_total = pl.pallas_call(
        kernel,
        out_shape=[shape(rows, width)] * slots
        + [shape(width, length, dtype=f32), shape(heads, length, dtype=f32)],
        in_specs=[SMEM, VMEM, VMEM, VMEM],
        out_specs=[VMEM] * (slots + 2),
        scratch_shapes=[pltpu.VMEM((length, width), bf16)],
        name="attend",
    )(plane.places, query, key, value)
    return pieces, out_t, log_total


def attend_back(heads, plane, query, key, value, cots, out_t, log_total):
    length, width = query.shape
    slots = plane.size
    rows = length // slots

    def kernel(places, q_ref, k_ref, v_ref, out_t_ref, log_ref, *refs):
        cot_refs, (g_ref, d_s, dk_s, dv_s, dq_t) = refs[:slots], refs[slots:]
        for slot in range(slots):
            d_s[pl.ds(pl.multiple_of(places[slot] * rows, rows), rows), :] = cot_refs[slot][...]
        dk_s[...] = jnp.zeros_like(dk_s)
        dv_s[...] = jnp.zeros_like(dv_s)
        for head in range(heads):
            cols = slice(head * HD, (head + 1) * HD)

            def block(index, until, head=head, cols=cols):
                at = pl.ds(index * ROWS, ROWS)
                query, cot = q_ref[at, cols], d_s[at, cols]
                delta = jnp.sum(cot.astype(f32).T * out_t_ref[cols, at], axis=0, keepdims=True)
                scores, kept = _scores(k_ref[0:until, cols], query, index * ROWS)
                weights = jnp.where(kept, jnp.exp(scores - log_ref[head : head + 1, at]), 0.0)
                d_weights = matmul(v_ref[0:until, cols], cot, 1, 1)
                d_scores = (weights * (d_weights - delta)).astype(bf16)
                dv_s[head, 0:until, :] += matmul(weights.astype(bf16), cot, 1, 0)
                dk_s[head, 0:until, :] += matmul(d_scores, query, 1, 0)
                dq_t[cols, at] = matmul(k_ref[0:until, cols].T, d_scores, 1, 0)

            _sweep(length, block)
        scale = 1.0 / math.sqrt(HD)
        g_ref[:, 0:width] = (dq_t[...] * scale).T.astype(bf16)
        for head in range(heads):
            at = width + head * HD
            g_ref[:, at : at + HD] = dk_s[head].astype(bf16)
            g_ref[:, at + width : at + width + HD] = dv_s[head].astype(bf16)

    return pl.pallas_call(
        kernel,
        out_shape=shape(length, 3 * width),
        in_specs=[SMEM] + [VMEM] * (5 + slots),
        out_specs=VMEM,
        scratch_shapes=[pltpu.VMEM((length, width), bf16)]
        + [pltpu.VMEM((heads, length, HD), f32)] * 2
        + [pltpu.VMEM((width, length), f32)],
        name="attend_back",
    )(plane.places, query, key, value, out_t, log_total, *cots)


def rows_spec(rows, width):
    return pl.BlockSpec((rows, width), lambda i: (i, 0))


def whole_spec(dims):
    return pl.BlockSpec(dims, lambda i: (0,) * len(dims), pipeline_mode=pl.Buffered(1))


def chip_spec(rows, width):
    return pl.BlockSpec((1, rows, width), lambda i: (i, 0, 0))


def project(plane, tokens, weight, gain, bias, bias_q, bias_v, span):
    length, width = tokens.shape
    rows = length // plane.chips

    def kernel(x_ref, w_ref, gain_ref, bias_ref, bq_ref, bv_ref, n_ref, q_ref, k_ref, v_ref):
        normal, _ = norm_parts(x_ref[...].astype(f32))
        normed = (normal * gain_ref[...] + bias_ref[...]).astype(bf16)
        n_ref[...] = normed
        made = matmul(normed, w_ref[:, 0 : 3 * span], 1, 0)
        queries = (made[:, 0:span] + bq_ref[...]).astype(bf16)
        q_ref[...] = queries * jnp.asarray(1.0 / math.sqrt(HD), bf16)
        k_ref[...] = made[:, span : 2 * span].astype(bf16)
        v_ref[...] = (made[:, 2 * span : 3 * span] + bv_ref[...]).astype(bf16)

    return pl.pallas_call(
        kernel,
        grid=(plane.chips,),
        out_shape=[shape(length, width)] + [shape(length, span)] * 3,
        in_specs=[rows_spec(rows, width)]
        + [whole_spec(v.shape) for v in (weight, gain, bias, bias_q, bias_v)],
        out_specs=[rows_spec(rows, width)] + [rows_spec(rows, span)] * 3,
        name="project",
    )(tokens, weight, gain, bias, bias_q, bias_v)


def split_store(core, part, scratch, mine_ref, theirs_ref):
    rows = scratch.shape[0] // 2
    scratch[...] = part.astype(bf16)
    mine_ref[0] = scratch[pl.ds(pl.multiple_of(core * rows, rows), rows), :]
    theirs_ref[0] = scratch[pl.ds(pl.multiple_of((1 - core) * rows, rows), rows), :]


def partial_rows(plane, left, weight, first, count, name):
    length = left.shape[0]
    width = weight.shape[0]
    rows = length // plane.chips

    def kernel(core, left_ref, w_ref, mine_ref, theirs_ref, scratch):
        part = matmul(left_ref[...], w_ref[:, first : first + count], 1, 1)
        split_store(core[0], part, scratch, mine_ref, theirs_ref)

    return pl.pallas_call(
        kernel,
        grid=(plane.chips,),
        out_shape=[shape(plane.chips, rows // 2, width)] * 2,
        in_specs=[SMEM, rows_spec(rows, count), whole_spec(weight.shape)],
        out_specs=[chip_spec(rows // 2, width)] * 2,
        scratch_shapes=[pltpu.VMEM((rows, width), bf16)],
        name=name,
    )(plane.me.astype(jnp.int32)[None] % 2, left, weight)


def feed_forward(plane, normed, cots, weight, bias):
    length, width = normed.shape
    rows = length // plane.chips
    part = weight.shape[1] // 2

    def kernel(core, n_ref, c_ref, w_ref, b_ref, a_ref, d_ref, sum_ref, mine_ref, theirs_ref, scratch):
        pre = matmul(n_ref[...], w_ref[:, 0:part], 1, 0) + b_ref[...]
        back = matmul(c_ref[...], w_ref[:, part : 2 * part], 1, 0)
        root = math.sqrt(2.0 / math.pi)
        square = pre * pre
        bend = jnp.tanh(root * (pre + 0.044715 * (pre * square)))
        half = 0.5 * (1.0 + bend)
        a_ref[...] = (pre * half).astype(bf16)
        slope = half + 0.5 * pre * (1.0 - bend * bend) * (root * (1.0 + 3 * 0.044715 * square))
        d_pre = (back * slope).astype(bf16)
        d_ref[...] = d_pre

        @pl.when(pl.program_id(0) == 0)
        def _():
            sum_ref[...] = jnp.zeros_like(sum_ref)

        sum_ref[...] += jnp.sum(d_pre.astype(f32), axis=0, keepdims=True)
        given = matmul(d_pre, w_ref[:, 0:part], 1, 1)
        split_store(core[0], given, scratch, mine_ref, theirs_ref)

    return pl.pallas_call(
        kernel,
        grid=(plane.chips,),
        out_shape=[shape(length, part)] * 2
        + [shape(1, part, dtype=f32)]
        + [shape(plane.chips, rows // 2, width)] * 2,
        in_specs=[SMEM, rows_spec(rows, width), rows_spec(rows, width)]
        + [whole_spec(weight.shape), whole_spec(bias.shape)],
        out_specs=[rows_spec(rows, part)] * 2
        + [pl.BlockSpec((1, part), lambda i: (0, 0))]
        + [chip_spec(rows // 2, width)] * 2,
        scratch_shapes=[pltpu.VMEM((rows, width), bf16)],
        name="feed_forward",
    )(plane.me.astype(jnp.int32)[None] % 2, normed, cots, weight, bias)


def branch_norm(plane, pieces, weights, tokens, bias, gain, bias_two):
    rows, width = tokens.shape
    slots = plane.size
    span = pieces[0].shape[1]
    part = weights.shape[2]

    def kernel(places, w_ref, x_ref, bias_ref, gain_ref, bias_two_ref, *refs):
        parts, (resid_ref, normed_ref, out_ref, o_s) = refs[:slots], refs[slots:]
        for slot in range(slots):
            o_s[places[slot]] = parts[slot][...]
        for j in range(slots):
            until = min((j + 1) * span, width)
            if j * span < width:
                out_ref[:, j * span : until] = o_s[j][:, 0 : until - j * span]
        out = out_ref[...]
        for j in range(slots):
            at = slice(j * part, (j + 1) * part)
            made = matmul(out, w_ref[j], 1, 0)
            resid_ref[:, at] = x_ref[:, at].astype(f32) + made + bias_ref[:, at]
        normal, _ = norm_parts(resid_ref[...])
        normed_ref[...] = (normal * gain_ref[...] + bias_two_ref[...]).astype(bf16)

    return pl.pallas_call(
        kernel,
        out_shape=[shape(rows, width, dtype=f32), shape(rows, width), shape(rows, width)],
        in_specs=[SMEM] + [VMEM] * (5 + slots),
        out_specs=[VMEM] * 3,
        scratch_shapes=[pltpu.VMEM((slots, rows, span), bf16)],
        name="branch_norm",
    )(plane.places, weights, tokens, bias, gain, bias_two, *pieces)


def branch_back(plane, terms, resid, cot, gain, weights, span):
    rows, width = resid.shape
    slots = plane.size
    part = weights.shape[2]
    count = len(terms)

    def kernel(places, resid_ref, cot_ref, gain_ref, w_ref, *refs):
        term_refs, refs = refs[:count], refs[count:]
        d_resid_ref, d_branch_ref, d_gain_ref, d_bias_ref = refs[:4]
        outs, d_s, padded = refs[4 : 4 + slots], refs[4 + slots], refs[5 + slots]
        total = term_refs[0][...]
        for term in term_refs[1:]:
            total = total + term[...].astype(f32)
        back, d_gain_ref[...], d_bias_ref[...] = norm_back(total, resid_ref[...], gain_ref[...])
        d_resid = cot_ref[...].astype(f32) + back
        d_resid_ref[...] = d_resid
        d_branch_ref[...] = d_resid.astype(bf16)
        given = jnp.zeros((rows, width), f32)
        for j in range(slots):
            at = slice(j * part, (j + 1) * part)
            given = given + matmul(d_branch_ref[:, at], w_ref[j], 1, 1)
        padded[...] = jnp.zeros_like(padded)
        padded[:, 0:width] = given.astype(bf16)
        for j in range(slots):
            d_s[j] = padded[:, j * span : (j + 1) * span]
        for slot in range(slots):
            outs[slot][...] = d_s[places[slot]]

    d_resid, d_branch, d_gain, d_bias, *pieces = pl.pallas_call(
        kernel,
        out_shape=[shape(rows, width, dtype=f32), shape(rows, width)]
        + [shape(1, width, dtype=f32)] * 2
        + [shape(rows, span)] * slots,
        in_specs=[SMEM] + [VMEM] * (4 + count),
        out_specs=[VMEM] * (4 + slots),
        scratch_shapes=[
            pltpu.VMEM((slots, rows, span), bf16),
            pltpu.VMEM((rows, slots * span), bf16),
        ],
        name="branch_back",
    )(plane.places, resid, cot, gain, weights, *terms)
    return d_resid, d_branch, d_gain, d_bias, pieces


def out_weight_parts(plane, left, right, part):
    rows, width = left.shape

    def kernel(core, left_ref, right_ref, mine_ref, theirs_ref, left_t, r_s):
        @pl.when(pl.program_id(0) == 0)
        def _():
            left_t[...] = left_ref[...].T
            for j in range(plane.size):
                r_s[j] = right_ref[:, j * part : (j + 1) * part]

        at = pl.program_id(0) * 2
        mine_ref[0] = matmul(left_t[...], r_s[at + core[0]], 1, 0).astype(bf16)
        theirs_ref[0] = matmul(left_t[...], r_s[at + 1 - core[0]], 1, 0).astype(bf16)

    return pl.pallas_call(
        kernel,
        grid=(plane.chips,),
        out_shape=[shape(plane.chips, width, part)] * 2,
        in_specs=[SMEM, whole_spec(left.shape), whole_spec(right.shape)],
        out_specs=[chip_spec(width, part)] * 2,
        scratch_shapes=[
            pltpu.VMEM((width, rows), bf16),
            pltpu.VMEM((plane.size, rows, part), bf16),
        ],
        name="out_weight_parts",
    )(plane.me.astype(jnp.int32)[None] % 2, left, right)


def columns_of(plane, pieces, layout):
    rows = pieces[0].shape[0]
    cols = pieces[0].shape[1]
    count = len(pieces)
    step = 80 if rows % 80 == 0 else rows
    widths = [sum(min(plane.size * n, most) for _, n, most in groups) for groups in layout]

    def kernel(places, *refs):
        parts, outs, scratch = refs[:count], refs[count:-1], refs[-1]
        for slot in range(count):
            scratch[places[slot]] = parts[slot][...]
        for out, groups in zip(outs, layout):
            base = 0
            for first, n, most in groups:
                for j in range(plane.size):
                    take = min(n, most - j * n)
                    if take > 0:
                        out[:, base + j * n : base + j * n + take] = scratch[
                            j, :, first : first + take
                        ].astype(f32)
                base += min(plane.size * n, most)

    return pl.pallas_call(
        kernel,
        grid=(rows // step,),
        out_shape=[shape(rows, w, dtype=f32) for w in widths],
        in_specs=[SMEM] + [rows_spec(step, cols)] * count,
        out_specs=[rows_spec(step, w) for w in widths],
        scratch_shapes=[pltpu.VMEM((count, step, cols), bf16)],
        name="columns_of",
    )(plane.places, *pieces)


def rows_of(plane, pieces):
    rows, cols = pieces[0].shape
    count = len(pieces)

    def kernel(places, *refs):
        parts, out, (buffer, sems) = refs[:count], refs[count], refs[count + 1 :]
        copies = []
        for slot in range(count):
            half = slot % 2
            if slot >= 2:
                copies[slot - 2].wait()
            buffer[half] = parts[slot][...].astype(f32)
            to = pl.ds(pl.multiple_of(places[slot] * rows, rows), rows)
            copies.append(pltpu.make_async_copy(buffer.at[half], out.at[to], sems.at[half]))
            copies[slot].start()
        for copy in copies[-2:]:
            copy.wait()

    return pl.pallas_call(
        kernel,
        out_shape=shape(count * rows, cols, dtype=f32),
        in_specs=[SMEM] + [VMEM] * count,
        out_specs=ANY,
        scratch_shapes=[pltpu.VMEM((2, rows, cols), f32), pltpu.SemaphoreType.DMA((2,))],
        name="rows_of",
    )(plane.places, *pieces)


def on_device(
    layer_in, out_cot, first_gain, first_bias, qkv_weight, qv_bias, out_weight, out_bias,
    second_gain, second_bias, fc_weight, fc_bias, proj_weight, proj_bias
):
    size = lax.axis_size("ctx")
    line = lax.axis_size("fsdp")
    plane = Plane(size)
    me = plane.me
    own_tokens, own_cot = layer_in[0], out_cot[0]
    rows, width = own_tokens.shape
    length = rows * size
    piece = width // line
    hidden = fc_weight.shape[1]
    part = hidden // size
    heads = -(-H // size)
    span = heads * HD
    spread = size * span
    out_part = width // size

    vectors = jnp.concatenate(
        [
            first_gain[None], first_bias[None], qv_bias, out_bias[None], second_gain[None],
            second_bias[None], proj_bias[None], fc_bias.reshape(-1, piece),
        ],
        axis=0,
    )
    count = vectors.shape[0]
    padded = jnp.pad(qkv_weight, ((0, 0), (0, spread - width)))
    packed = [
        lax.dynamic_slice_in_dim(padded, i * width + me * span, span, axis=1) for i in range(3)
    ]
    packed.append(lax.dynamic_slice_in_dim(out_weight, me * out_part, out_part, axis=1))
    packed.append(vectors.T)
    used = 3 * span + out_part + count
    first_cols = -(-used // 128) * 128
    packed.append(jnp.zeros((piece, first_cols - used), bf16))
    first_set = line_gather(jnp.concatenate(packed, axis=1), line)

    second_set = jnp.concatenate(
        [
            lax.dynamic_slice_in_dim(fc_weight, me * part, part, axis=1),
            lax.dynamic_slice_in_dim(proj_weight, me * part, part, axis=0).T,
        ],
        axis=1,
    )
    second_set = lax.all_gather(second_set, "fsdp", axis=0, tiled=True)

    both = plane.gather(jnp.concatenate([own_tokens, own_cot], axis=0))
    both = plane.collect([v.reshape(2, rows, width) for v in both])
    all_tokens = both[:, 0].reshape(length, width)
    all_cot = both[:, 1].reshape(length, width)

    vectors = first_set[:, 3 * span + out_part : used].T.astype(f32)
    gain_one, bias_one, bias_q, bias_v, bias_out, gain_two, bias_two, bias_proj = (
        vectors[i : i + 1] for i in range(8)
    )
    bias_fc = vectors[8:].reshape(-1, line, piece).transpose(1, 0, 2).reshape(1, hidden)
    bias_fc = lax.dynamic_slice_in_dim(bias_fc, me * part, part, axis=1)

    def heads_of(vector):
        vector = jnp.pad(vector, ((0, 0), (0, spread - width)))
        return lax.dynamic_slice_in_dim(vector, me * span, span, axis=1)

    out_cols = plane.collect(plane.gather(first_set[:, 3 * span : 3 * span + out_part]))

    normed_one, queries, keys, values = project(
        plane, all_tokens, first_set, gain_one, bias_one, heads_of(bias_q), heads_of(bias_v), span
    )
    pieces, attn_t, log_total = attend(heads, plane, queries, keys, values)
    pieces = plane.exchange(pieces)
    resid, normed_two, attn_out = branch_norm(
        plane, pieces, out_cols, own_tokens, bias_out, gain_two, bias_two
    )

    normed_two = plane.collect(plane.gather(normed_two)).reshape(length, width)
    activated, d_pre, grad_bias_fc, mine, theirs = feed_forward(
        plane, normed_two, all_cot, second_set, bias_fc
    )
    d_norm_two = plane.scatter(mine, theirs)
    grad_proj = matmul(all_cot, activated, 0, 0).astype(bf16).reshape(line, piece, part)
    grad_proj = line_scatter(grad_proj)
    grad_fc = matmul(normed_two, d_pre, 0, 0).astype(bf16).reshape(line, piece, part)
    grad_fc = line_scatter(grad_fc)
    mine, theirs = partial_rows(plane, activated, second_set, part, part, "mlp_out")
    mlp_out = plane.scatter(mine, theirs)
    layer_out = resid + bias_proj
    for term in mlp_out:
        layer_out = layer_out + term.astype(f32)
    layer_out = layer_out.astype(bf16)[None]

    d_resid, d_branch, grad_gain_two, grad_bias_two, pieces = branch_back(
        plane, d_norm_two, resid, own_cot, gain_two, out_cols, span
    )
    cots = plane.exchange(pieces)
    grads = attend_back(heads, plane, queries, keys, values, cots, attn_t, log_total)
    mine, theirs = partial_rows(plane, grads, first_set, 0, 3 * span, "d_norm_one")
    d_norm_one = plane.scatter(mine, theirs)
    total = d_norm_one[0]
    for term in d_norm_one[1:]:
        total = total + term.astype(f32)
    d_in, grad_gain_one, grad_bias_one = norm_back(total, own_tokens.astype(f32), gain_one)
    grad_in = (d_resid + d_in).astype(bf16)[None]

    mine, theirs = out_weight_parts(plane, attn_out, d_branch, out_part)
    grad_out = plane.scatter(mine, theirs)
    total = grad_out[0]
    for term in grad_out[1:]:
        total = total + term.astype(f32)
    grad_qkv = matmul(normed_one, grads, 0, 0)
    third_set = jnp.concatenate(
        [
            grad_qkv.astype(bf16),
            total.astype(bf16),
            jnp.zeros((width, first_cols - 3 * span - out_part), bf16),
        ],
        axis=1,
    )
    third_set = line_scatter(third_set.reshape(line, piece, first_cols))

    grad_proj = rows_of(plane, plane.gather(grad_proj.T))
    (grad_fc,) = columns_of(plane, plane.gather(grad_fc), [[(0, part, hidden)]])
    grad_qkv, grad_out = columns_of(
        plane,
        plane.gather(third_set),
        [[(i * span, span, width) for i in range(3)], [(3 * span, out_part, width)]],
    )

    def summed(value):
        return jnp.sum(value.astype(f32), axis=0, keepdims=True)

    vectors = jnp.concatenate(
        [
            grad_gain_one, grad_bias_one, summed(d_branch), grad_gain_two, grad_bias_two,
            summed(own_cot), summed(grads[:, :span]), summed(grads[:, 2 * span :]),
            grad_bias_fc,
        ],
        axis=1,
    )
    vectors = plane.collect(plane.gather(vectors))[:, 0]
    by_token = jnp.sum(vectors[:, : 6 * width], axis=0).reshape(6, line, piece)
    vectors = vectors[:, 6 * width :]
    bias_parts = jnp.stack(
        [vectors[:, i * span : (i + 1) * span].reshape(spread)[:width] for i in range(2)]
    ).reshape(2, line, piece)
    hidden_part = vectors[:, 2 * span :].reshape(line, hidden // line)
    parts = jnp.concatenate(
        [
            by_token.transpose(1, 0, 2).reshape(line, 6 * piece),
            bias_parts.transpose(1, 0, 2).reshape(line, 2 * piece),
            hidden_part,
        ],
        axis=1,
    )
    at = lax.axis_index("fsdp")
    final = lax.dynamic_index_in_dim(parts, at, 0, keepdims=False)
    for step in range(1, line):
        sent = lax.dynamic_index_in_dim(parts, (at + step) % line, 0, keepdims=False)
        final = final + lax.ppermute(sent, "fsdp", [(i, (i + step) % line) for i in range(line)])
    singles = [final[i * piece : (i + 1) * piece] for i in range(8)]
    return (
        layer_out,
        grad_in,
        singles[0],
        singles[1],
        grad_qkv,
        jnp.stack(singles[6:8]),
        grad_out,
        singles[2],
        singles[3],
        singles[4],
        grad_fc,
        final[8 * piece :],
        grad_proj,
        singles[5],
    )


def solution(mesh):
    by_width = P("fsdp")
    tokens = P("fsdp", "ctx", None)
    matrix = P("fsdp", None)
    across = P(None, "fsdp")
    params = (
        by_width, by_width, matrix, across, matrix, by_width, by_width, by_width, matrix, by_width,
        across, by_width,
    )
    return jax.shard_map(
        on_device,
        mesh=mesh,
        in_specs=(tokens, tokens) + params,
        out_specs=(tokens, tokens) + params,
        check_vma=False,
    )
```
